32 devices in a mesh: pert: 2 (over y), band: 16 (over z, x, core).
Axes of the slice: x: 2, y: 2, z: 4, core: 2. Of those that a mesh axis runs over, the one named last changes fastest.
Arguments:
- response: bfloat16 [1024, 12288], P('pert', 'band'), parts along dimension 0, may hold values from -6 to 6
- orbitals: bfloat16 [512, 12288], P(None, 'band'), may hold values from -6 to 6
- projectors: bfloat16 [2048, 12288], P(None, 'band'), may hold values from -6 to 6
- potential: float32 [12288], P('band'), may hold values from -1 to 1
- perturbing: float32 [24576], P(('pert', 'band')), parts along dimension 0, may hold values from -6 to 6
- energies: float32 [512], replicated, may hold values from -1 to -0.2
- window_start: int32 [512], replicated, may hold values from 0 to 31, as said below
- block_count: int32 [512], replicated, may hold values from 1 to 9, as said below
Outputs:
- updated_response: bfloat16 [1024, 12288], P('pert', 'band'), parts along dimension 0
- residual: bfloat16 [1024, 12288], P('pert', 'band'), parts along dimension 0
The draws below stay inside these ranges and needn't reach their ends.
There are 2 independent parts, one for each index of `pert`. The reference program is written for one: setup_inputs(seed, part) draws one part's arguments, and reference() takes and returns one part's arrays. A program takes and returns all parts, laid end to end along the dimension named above; an argument that names none is the same for every part. Nothing has to cross between parts.
Inputs may be any that keep to these rules, and one draw needn't show every extreme that they name: `window_start`: band n lies in block n // 16. Each band's window contains its own block and starts at most 4 blocks below it. `block_count`: each band's window ends at most 4 blocks above its own block and never past block 31.
All inputs are finite; a program needn't handle non-finite values.
Results may differ from the reference program's by a relative error of at most 0.0041.
Values may be sent and summed in bfloat16 or wider, within the bound.
A program may use at most 128 MiB of HBM per device.

```python
import math
import jax
import jax.numpy as jnp

GY = 8
GZ = 16
NOCC = 2048
NBW = 512
NBLK = 32
REACH = 4
GX = 96
CELLS = 12288
BLK = 16


def window_parts(key):
    base_key = jax.random.fold_in(key, 11)
    lower_reach = jax.random.randint(jax.random.fold_in(base_key, 1), (NBW,), 0, REACH + 1)
    upper_reach = jax.random.randint(jax.random.fold_in(base_key, 2), (NBW,), 0, REACH + 1)
    band_index = jnp.arange(NBW, dtype=jnp.int32)
    own_block = band_index // BLK
    widest = band_index == NBLK // 2 * BLK
    lower_reach = jnp.where(widest, REACH, lower_reach)
    upper_reach = jnp.where(widest, REACH, upper_reach)
    final_band = band_index == NBW - 1
    lower_reach = jnp.where(final_band, 0, lower_reach)
    first_block = jnp.maximum(own_block - lower_reach, 0)
    last_block = jnp.minimum(own_block + upper_reach, NBLK - 1)
    return (first_block.astype(jnp.int32), (last_block - first_block + 1).astype(jnp.int32))


def draw_window_start(key, part):
    return window_parts(key)[0]


def draw_block_count(key, part):
    return window_parts(key)[1]


def level_of(stream_key, extent, cuts, smallest, largest):
    def one(dim, blocks):
        draws = jax.random.uniform(jax.random.fold_in(jax.random.fold_in(stream_key, 6), dim), (blocks,), jnp.float32, smallest / len(cuts), largest / len(cuts))
        return jnp.repeat(jnp.exp(draws), extent[dim] // blocks).reshape((-1,) + (1,) * (len(extent) - dim - 1))

    gain = one(*cuts[0])
    for cut in cuts[1:]:
        gain = gain * one(*cut)
    return gain


def centred(key, dims, deviation, limit, shards=(), held_as=jnp.bfloat16):
    array = deviation * jax.random.normal(key, dims, jnp.float32)
    if shards:
        array = array * level_of(key, dims, shards, -0.22, 0.18)
    return jnp.clip(array, -limit, limit).astype(held_as)


def setup_inputs(seed: int = 0, part: int = 0) -> dict:
    splits = jax.random.split(jax.random.key(seed), 9)
    part_splits = jax.random.split(jax.random.fold_in(splits[8], part), 9)
    return {
        "response": centred(part_splits[0], (NBW, CELLS), 1.0, 6.0, ((1, 16),)),
        "orbitals": centred(splits[1], (NBW, CELLS), 1.0, 6.0, ((1, 16),)),
        "projectors": centred(splits[2], (NOCC, CELLS), 1.0, 6.0, ((1, 16),)),
        "potential": jnp.clip(jax.random.uniform(splits[3], (CELLS,), jnp.float32, -1.0, 1.0) * level_of(splits[3], (CELLS,), ((0, 16),), -0.4, 0.0), -1.0, 1.0),
        "perturbing": centred(part_splits[4], (CELLS,), 1.0, 6.0, ((0, 16),), jnp.float32),
        "energies": jnp.clip(jax.random.uniform(splits[5], (NBW,), jnp.float32, -1.0, -0.2), -1.0, -0.2),
        "window_start": draw_window_start(jax.random.fold_in(splits[8], 71), part),
        "block_count": draw_block_count(jax.random.fold_in(splits[8], 71), part),
    }


COEFFS = (-5369.0 / 1800.0, 12.0 / 7.0, -15.0 / 56.0, 10.0 / 189.0, -1.0 / 112.0, 2.0 / 1925.0, -1.0 / 16632.0)
KINETIC = 0.125
STEP_SIZE = 0.3

def laplacian(grid_field):
    result = 3.0 * COEFFS[0] * grid_field
    for axis_number in (1, 2, 3):
        for offset in range(1, 7):
            result = result + COEFFS[offset] * (jnp.roll(grid_field, offset, axis_number) + jnp.roll(grid_field, -offset, axis_number))
    return result

def reference(response, orbitals, projectors, potential, perturbing, energies, window_start, block_count):
    cells = GX * GY * GZ
    ace_scale = 1.0 / math.sqrt(cells * NOCC)
    window_scale = 1.0 / math.sqrt(cells * NBW)
    response_wide = response.astype(jnp.float32)
    kinetic = -KINETIC * laplacian(response_wide.reshape(NBW, GX, GY, GZ)).reshape(NBW, cells)
    ace_intersection = (jnp.dot(response, projectors.T, preferred_element_type=jnp.float32) * ace_scale).astype(jnp.bfloat16)
    ace_term = -jnp.dot(ace_intersection, projectors, preferred_element_type=jnp.float32)
    applied = kinetic + potential[None, :] * response_wide + ace_term - energies[:, None] * response_wide
    orbitals_wide = orbitals.astype(jnp.float32)
    unprojected = -(perturbing[None, :] * orbitals_wide) - applied
    unprojected_low = unprojected.astype(jnp.bfloat16)
    intersections = (jnp.dot(unprojected_low, orbitals.T, preferred_element_type=jnp.float32) * window_scale).astype(jnp.bfloat16)
    block_ids = jnp.arange(NBW, dtype=jnp.int32) // (NBW // NBLK)
    lowest = window_start[:, None]
    highest = window_start[:, None] + block_count[:, None] - 1
    inside = (block_ids[None, :] >= lowest) & (block_ids[None, :] <= highest)
    intersections = jnp.where(inside, intersections, jnp.zeros_like(intersections))
    residual_wide = unprojected - jnp.dot(intersections, orbitals, preferred_element_type=jnp.float32)
    updated_response = (response_wide + STEP_SIZE * residual_wide).astype(jnp.bfloat16)
    return (updated_response, residual_wide.astype(jnp.bfloat16))
```

```python
import functools
import math

import jax
import jax.numpy as jnp
import numpy as np
from jax import lax
from jax.experimental import pallas as pl
from jax.experimental.pallas import tpu as pltpu
from jax.sharding import PartitionSpec as P

GY = 8
GZ = 16
NBLK = 32
REACH = 4


COEFFS = (
    -5369.0 / 1800.0,
    12.0 / 7.0,
    -15.0 / 56.0,
    10.0 / 189.0,
    -1.0 / 112.0,
    2.0 / 1925.0,
    -1.0 / 16632.0,
)
KINETIC = 0.125
STEP_SIZE = 0.3
HALO = 6
NT = (((1,), (1,)), ((), ()))
WIDTH = 256
ROWS = 32
ROW_SHARES = 8


CONTRACT_CELLS = (((1,), (1,)), ((), ()))


def padded_2(cells, sides, width):
    for axis, dim in sides:
        count = lax.axis_size(axis)
        head = lax.slice_in_dim(cells, 0, width, axis=dim)
        tail = lax.slice_in_dim(cells, cells.shape[dim] - width, cells.shape[dim], axis=dim)
        cells = jnp.concatenate(
            [
                lax.ppermute(tail, axis, [(i, (i + 1) % count) for i in range(count)]),
                cells,
                lax.ppermute(head, axis, [((i + 1) % count, i) for i in range(count)]),
            ],
            axis=dim,
        )
    return cells


def slab_laplacian(padded, depth):
    centre = padded[:, 6 : 6 + depth]
    result = 3.0 * COEFFS[0] * centre
    for offset in range(1, 7):
        result = result + COEFFS[offset] * (
            padded[:, 6 + offset : 6 + offset + depth] + padded[:, 6 - offset : 6 - offset + depth]
        )
    for axis_number in (2, 3):
        for offset in range(1, 7):
            result = result + COEFFS[offset] * (
                jnp.roll(centre, offset, axis_number) + jnp.roll(centre, -offset, axis_number)
            )
    return result


def plain_shards(
    response, orbitals, projectors, potential, perturbing, energies, window_start, block_count
):
    band_rows = response.shape[0]
    local_cells = response.shape[1]
    devices = lax.axis_size("band")
    cells = local_cells * devices
    plane = GY * GZ
    depth = local_cells // plane
    ace_scale = 1.0 / math.sqrt(cells * projectors.shape[0])
    window_scale = 1.0 / math.sqrt(cells * band_rows)
    padded = padded_2(response.reshape(band_rows, depth, plane), (("band", 1),), 6)
    padded_wide = padded.astype(jnp.float32).reshape(band_rows, depth + 12, GY, GZ)
    kinetic = -KINETIC * slab_laplacian(padded_wide, depth).reshape(band_rows, local_cells)
    response_wide = response.astype(jnp.float32)
    picked = response
    share = lax.psum_scatter(
        lax.dot_general(picked, projectors, CONTRACT_CELLS, preferred_element_type=jnp.float32),
        "band",
        scatter_dimension=0,
        tiled=True,
    )
    ace_intersection = lax.all_gather(
        (share * ace_scale).astype(jnp.bfloat16), "band", axis=0, tiled=True
    )
    ace_term = -jnp.dot(ace_intersection, projectors, preferred_element_type=jnp.float32)
    applied = (
        kinetic + potential[None, :] * response_wide + ace_term - energies[:, None] * response_wide
    )
    orbitals_wide = orbitals.astype(jnp.float32)
    unprojected = -(perturbing[None, :] * orbitals_wide) - applied
    unprojected_low = unprojected.astype(jnp.bfloat16)
    picked = unprojected_low
    window_share = lax.psum_scatter(
        lax.dot_general(picked, orbitals, CONTRACT_CELLS, preferred_element_type=jnp.float32),
        "band",
        scatter_dimension=0,
        tiled=True,
    )
    window_intersection = lax.all_gather(
        (window_share * window_scale).astype(jnp.bfloat16), "band", axis=0, tiled=True
    )
    block_ids = jnp.arange(band_rows, dtype=jnp.int32) // (band_rows // NBLK)
    lowest = window_start[:, None]
    highest = window_start[:, None] + block_count[:, None] - 1
    inside = (block_ids[None, :] >= lowest) & (block_ids[None, :] <= highest)
    window_intersection = jnp.where(
        inside, window_intersection, jnp.zeros_like(window_intersection)
    )
    residual_wide = unprojected - jnp.dot(
        window_intersection, orbitals, preferred_element_type=jnp.float32
    )
    updated_response = (response_wide + STEP_SIZE * residual_wide).astype(jnp.bfloat16)
    return (updated_response, residual_wide.astype(jnp.bfloat16))


def plane_operator():
    plane = GY * GZ
    op = np.zeros((plane, plane), np.float64)
    for y in range(GY):
        for z in range(GZ):
            out = y * GZ + z
            op[out, out] += 3.0 * COEFFS[0]
            for k in range(1, HALO + 1):
                for sign in (-k, k):
                    op[((y + sign) % GY) * GZ + z, out] += COEFFS[k]
                    op[y * GZ + (z + sign) % GZ, out] += COEFFS[k]
    return (KINETIC * op).astype(np.float32)


def kernel(
    count, groups, ace_scale, window_scale,
    resp, orb, proj, pot, pert, energies, first, blocks, op_hi, op_lo,
    updated, residual,
    halo_l, halo_r, unp, low, acc, c_send, c_recv, x_send, x_recv, z_send, z_recv, full,
    send_sem, recv_sem, halo_send, halo_recv,
):
    rows, cells = resp.shape
    plane = GY * GZ
    depth = cells // plane
    half, quarter = rows // 2, rows // 4
    share = quarter // groups
    chunks = proj.shape[0] // WIDTH

    me = lax.axis_index("band")
    core = me % 2
    across = (me // 2) % 2
    level = me // 4
    left, right = (me + count - 1) % count, (me + 1) % count
    core_peer = me + 1 - 2 * core
    x_peer = me + 2 - 4 * across
    z_levels = [(level + k) % groups for k in range(1, groups)]
    z_peers = [v * 4 + me % 4 for v in z_levels]

    def remote(src, dst, send, recv, device):
        return pltpu.make_async_remote_copy(
            src_ref=src, dst_ref=dst, send_sem=send, recv_sem=recv,
            device_id={"band": device}, device_id_type=pl.DeviceIdType.MESH,
        )

    partners = [left, right, core_peer, x_peer] + z_peers
    barrier = pltpu.get_barrier_semaphore()
    for device in partners:
        pl.semaphore_signal(
            barrier, inc=1, device_id={"band": device}, device_id_type=pl.DeviceIdType.MESH
        )
    pl.semaphore_wait(barrier, len(partners))

    width = HALO * plane
    halos = [
        remote(resp.at[:, cells - width :], halo_l, halo_send.at[0], halo_recv.at[0], right),
        remote(resp.at[:, :width], halo_r, halo_send.at[1], halo_recv.at[1], left),
    ]

    core_row = pl.multiple_of(core * half, half)
    other_row = pl.multiple_of((1 - core) * half, half)
    x_row = pl.multiple_of(core * half + across * quarter, quarter)
    own_row = pl.multiple_of(core * half + across * quarter + level * share, share)
    x_mine = pl.multiple_of(across * quarter, quarter)
    x_other = pl.multiple_of((1 - across) * quarter, quarter)

    nz = groups - 1
    copies = {}

    def begin(j, kind, src, dst, device):
        copy = remote(src, dst, send_sem.at[j, kind], recv_sem.at[j, kind], device)
        copy.start()
        copies[j, kind] = copy

    def partial(j, h, row):
        if j < chunks:
            return lax.dot_general(
                resp[pl.ds(row, half), :], proj[j * WIDTH : (j + 1) * WIDTH, :], NT,
                preferred_element_type=jnp.float32,
            )
        return jnp.concatenate(
            [
                lax.dot_general(
                    low[pl.ds(pl.multiple_of(row + g * quarter, quarter), quarter), :],
                    orb[pl.ds(window(h, g), WIDTH), :], NT,
                    preferred_element_type=jnp.float32,
                )
                for g in range(2)
            ],
            axis=0,
        )

    reach = REACH * (rows // NBLK)

    def window(h, g):
        start = h * (2 * quarter - reach) if g == 0 else quarter - reach + h * (quarter + reach)
        return pl.multiple_of(start, reach)

    def stage_0(j):
        c_send[j] = partial(j, 1 - core, other_row).astype(jnp.bfloat16)
        begin(j, 0, c_send.at[j], c_recv.at[j], core_peer)
        acc[j] = partial(j, core, core_row)

    def stage_1(j):
        copies[j, 0].wait_recv()
        x_send[j] = (
            acc[j, pl.ds(x_other, quarter), :]
            + c_recv[j, pl.ds(x_other, quarter), :].astype(jnp.float32)
        ).astype(jnp.bfloat16)
        begin(j, 1, x_send.at[j], x_recv.at[j], x_peer)

    def stage_2(j):
        copies[j, 1].wait_recv()
        total = (
            acc[j, pl.ds(x_mine, quarter), :]
            + c_recv[j, pl.ds(x_mine, quarter), :].astype(jnp.float32)
            + x_recv[j].astype(jnp.float32)
        )
        acc[j, :quarter, :] = total
        z_send[j] = total.astype(jnp.bfloat16)
        for k in range(nz):
            begin(
                j, 2 + k,
                z_send.at[j, pl.ds(pl.multiple_of(z_levels[k] * share, share), share), :],
                z_recv.at[j, k], z_peers[k],
            )

    def stage_3(j):
        total = acc[j, pl.ds(pl.multiple_of(level * share, share), share), :]
        for k in range(nz):
            copies[j, 2 + k].wait_recv()
            total = total + z_recv[j, k].astype(jnp.float32)
        scale = ace_scale if j < chunks else window_scale
        full[j, pl.ds(own_row, share), :] = (total * scale).astype(jnp.bfloat16)
        piece = full.at[j, pl.ds(own_row, share), :]
        for k in range(nz):
            begin(j, 2 + nz + k, piece, piece, z_peers[k])

    def stage_4(j):
        for k in range(nz):
            copies[j, 2 + nz + k].wait_recv()
        piece = full.at[j, pl.ds(x_row, quarter), :]
        begin(j, 2 + 2 * nz, piece, piece, x_peer)

    def stage_5(j):
        copies[j, 2 + 2 * nz].wait_recv()
        piece = full.at[j, pl.ds(core_row, half), :]
        begin(j, 3 + 2 * nz, piece, piece, core_peer)

    def stage_6(j):
        copies[j, 3 + 2 * nz].wait_recv()
        if j < chunks:
            for lo in range(0, cells, WIDTH):
                unp[:, lo : lo + WIDTH] += jnp.dot(
                    full[j], proj[j * WIDTH : (j + 1) * WIDTH, lo : lo + WIDTH],
                    preferred_element_type=jnp.float32,
                )

    stages = [stage_0, stage_1, stage_2, stage_3, stage_4, stage_5, stage_6]

    def in_plane():
        for p in range(depth):
            cut = resp[:, p * plane : (p + 1) * plane]
            unp[:, p * plane : (p + 1) * plane] = jnp.dot(
                cut, op_hi[...], preferred_element_type=jnp.float32
            ) + jnp.dot(cut, op_lo[...], preferred_element_type=jnp.float32)

    columns = {}

    def column(ref):
        return jnp.broadcast_to(ref[...].astype(jnp.float32), (plane, rows)).T

    def local_terms(begin_row, end_row):
        @pl.loop(begin_row // ROWS, end_row // ROWS)
        def _(i):
            at = pl.ds(pl.multiple_of(i * ROWS, ROWS), ROWS)
            planes = [
                resp[at, p * plane : (p + 1) * plane].astype(jnp.float32) for p in range(depth)
            ]
            energy = columns["energies"][at, :]
            for p in range(depth):
                cut = slice(p * plane, (p + 1) * plane)
                value = unp[at, cut] + (energy - pot[:, cut]) * planes[p]
                value = value - pert[:, cut] * orb[at, cut].astype(jnp.float32)
                for k in range(1, HALO + 1):
                    for q in (p - k, p + k):
                        if 0 <= q < depth:
                            value = value + (KINETIC * COEFFS[k]) * planes[q]
                unp[at, cut] = value

    def halo_terms():
        for copy in halos:
            copy.wait_recv()

        @pl.loop(0, rows // ROWS)
        def _(i):
            at = pl.ds(pl.multiple_of(i * ROWS, ROWS), ROWS)
            before = [
                halo_l[at, p * plane : (p + 1) * plane].astype(jnp.float32) for p in range(HALO)
            ]
            after = [
                halo_r[at, p * plane : (p + 1) * plane].astype(jnp.float32) for p in range(HALO)
            ]
            for p in range(depth):
                value = None
                for k in range(1, HALO + 1):
                    if p - k < 0:
                        term = (KINETIC * COEFFS[k]) * before[HALO + p - k]
                        value = term if value is None else value + term
                    if p + k >= depth:
                        term = (KINETIC * COEFFS[k]) * after[p + k - depth]
                        value = term if value is None else value + term
                if value is not None:
                    unp[at, p * plane : (p + 1) * plane] += value

    slots = chunks + len(stages) - 1
    halo_slot = chunks + 3
    for t in range(slots):
        if t == 0:
            stage_0(0)
            for copy in halos:
                copy.start()
            in_plane()
            acc[chunks, :, :plane] = column(energies)[:half]
            acc[chunks, :, plane : 2 * plane] = column(energies)[half:]
            continue
        for s in range(len(stages) - 1, -1, -1):
            j = t - s
            if 0 <= j < chunks:
                stages[s](j)
        if 1 <= t <= 2:
            columns["energies"] = _HalfView(acc, chunks, (t - 1) * half, plane, t - 1)
            local_terms((t - 1) * half, t * half)
        if t == halo_slot:
            halo_terms()

    for lo in range(0, rows, quarter):
        low[lo : lo + quarter, :] = unp[lo : lo + quarter, :].astype(jnp.bfloat16)
    for stage in stages:
        stage(chunks)

    block = rows // NBLK
    start_col = column(first)
    end_col = start_col + column(blocks)
    for g in range(4):
        at = slice(g * quarter, (g + 1) * quarter)
        start = (0, quarter - reach, 2 * quarter - reach, rows - WIDTH)[g]
        lanes = (lax.broadcasted_iota(jnp.int32, (quarter, plane), 1)).astype(jnp.float32)
        cuts = []
        for lo in range(0, WIDTH, plane):
            ids = jnp.floor((lanes + float(start + lo)) * (1.0 / block))
            inside = (ids >= start_col[at]) & (ids < end_col[at])
            cuts.append(
                jnp.where(inside, full[chunks, at, lo : lo + plane].astype(jnp.float32), 0.0)
            )
        weights = jnp.concatenate(cuts, axis=1).astype(jnp.bfloat16)
        for lo in range(0, cells, WIDTH):
            wide = unp[at, lo : lo + WIDTH] - jnp.dot(
                weights, orb[start : start + WIDTH, lo : lo + WIDTH],
                preferred_element_type=jnp.float32,
            )
            residual[at, lo : lo + WIDTH] = wide.astype(jnp.bfloat16)
            updated[at, lo : lo + WIDTH] = (
                resp[at, lo : lo + WIDTH].astype(jnp.float32) + STEP_SIZE * wide
            ).astype(jnp.bfloat16)

    for copy in copies.values():
        copy.wait_send()
    for copy in halos:
        copy.wait_send()


class _HalfView:
    def __init__(self, ref, index, offset, plane, part):
        self.ref, self.index, self.offset, self.plane, self.part = ref, index, offset, plane, part

    def __getitem__(self, key):
        at = key[0]
        lo = self.part * self.plane
        return self.ref[
            self.index,
            pl.ds(pl.multiple_of(at.start - self.offset, ROWS), at.size),
            lo : lo + self.plane,
        ]


def shards(
    response, orbitals, projectors, potential, perturbing, energies, window_start, block_count
):
    rows, local = response.shape
    count = lax.axis_size("band")
    cells = local * count
    groups = count // 4
    chunks = projectors.shape[0] // WIDTH
    half, quarter = rows // 2, rows // 4
    share = quarter // groups
    kinds = 4 + 2 * (groups - 1)
    op = plane_operator()
    op_hi = jnp.asarray(op).astype(jnp.bfloat16)
    op_lo = (jnp.asarray(op) - op_hi.astype(jnp.float32)).astype(jnp.bfloat16)
    halo = (rows, HALO * GY * GZ)
    low = jnp.bfloat16
    total = chunks + 1
    vmem = pl.BlockSpec(memory_space=pltpu.VMEM)
    return pl.pallas_call(
        functools.partial(
            kernel, count, groups,
            1.0 / math.sqrt(cells * projectors.shape[0]), 1.0 / math.sqrt(cells * rows),
        ),
        out_shape=(
            jax.ShapeDtypeStruct(response.shape, low),
            jax.ShapeDtypeStruct(response.shape, low),
        ),
        in_specs=[vmem] * 10,
        out_specs=(vmem, vmem),
        scratch_shapes=[
            pltpu.VMEM(halo, low),
            pltpu.VMEM(halo, low),
            pltpu.VMEM((rows, local), jnp.float32),
            pltpu.VMEM((rows, local), low),
            pltpu.VMEM((total, half, WIDTH), jnp.float32),
            pltpu.VMEM((total, half, WIDTH), low),
            pltpu.VMEM((total, half, WIDTH), low),
            pltpu.VMEM((total, quarter, WIDTH), low),
            pltpu.VMEM((total, quarter, WIDTH), low),
            pltpu.VMEM((total, quarter, WIDTH), low),
            pltpu.VMEM((total, groups - 1, share, WIDTH), low),
            pltpu.VMEM((total, rows, WIDTH), low),
            pltpu.SemaphoreType.DMA((total, kinds)),
            pltpu.SemaphoreType.DMA((total, kinds)),
            pltpu.SemaphoreType.DMA((2,)),
            pltpu.SemaphoreType.DMA((2,)),
        ],
        compiler_params=pltpu.CompilerParams(
            collective_id=0, has_side_effects=True, vmem_limit_bytes=56 * 1024 * 1024
        ),
    )(
        response, orbitals, projectors,
        potential[None, :], perturbing[None, :],
        energies[None, :], window_start[None, :], block_count[None, :],
        op_hi, op_lo,
    )


def solution(mesh):
    groups = mesh.shape["band"] // 4
    fits = groups * 4 == mesh.shape["band"] and ROW_SHARES % groups == 0
    in_specs = (
        P("pert", "band"),
        P(None, "band"),
        P(None, "band"),
        P("band"),
        P(("pert", "band")),
        P(),
        P(),
        P(),
    )
    out_specs = (P("pert", "band"), P("pert", "band"))
    return jax.shard_map(shards if fits else plain_shards, mesh=mesh, in_specs=in_specs, out_specs=out_specs, check_vma=False)
```

```python
import functools
import math

import jax
import jax.numpy as jnp
import numpy as np
from jax import lax
from jax.experimental import pallas as pl
from jax.experimental.pallas import tpu as pltpu
from jax.sharding import PartitionSpec as P

GY = 8
GZ = 16
NBLK = 32
REACH = 4


COEFFS = (
    -5369.0 / 1800.0,
    12.0 / 7.0,
    -15.0 / 56.0,
    10.0 / 189.0,
    -1.0 / 112.0,
    2.0 / 1925.0,
    -1.0 / 16632.0,
)
KINETIC = 0.125
STEP_SIZE = 0.3
HALO = 6
NT = (((1,), (1,)), ((), ()))
WIDTH = 256
ROWS = 32
ROW_SHARES = 8
DELAYS = (0, 1, 3, 5, 7, 9, 10)


CONTRACT_CELLS = (((1,), (1,)), ((), ()))


def padded_2(cells, sides, width):
    for axis, dim in sides:
        count = lax.axis_size(axis)
        head = lax.slice_in_dim(cells, 0, width, axis=dim)
        tail = lax.slice_in_dim(cells, cells.shape[dim] - width, cells.shape[dim], axis=dim)
        cells = jnp.concatenate(
            [
                lax.ppermute(tail, axis, [(i, (i + 1) % count) for i in range(count)]),
                cells,
                lax.ppermute(head, axis, [((i + 1) % count, i) for i in range(count)]),
            ],
            axis=dim,
        )
    return cells


def slab_laplacian(padded, depth):
    centre = padded[:, 6 : 6 + depth]
    result = 3.0 * COEFFS[0] * centre
    for offset in range(1, 7):
        result = result + COEFFS[offset] * (
            padded[:, 6 + offset : 6 + offset + depth] + padded[:, 6 - offset : 6 - offset + depth]
        )
    for axis_number in (2, 3):
        for offset in range(1, 7):
            result = result + COEFFS[offset] * (
                jnp.roll(centre, offset, axis_number) + jnp.roll(centre, -offset, axis_number)
            )
    return result


def plain_shards(
    response, orbitals, projectors, potential, perturbing, energies, window_start, block_count
):
    band_rows = response.shape[0]
    local_cells = response.shape[1]
    devices = lax.axis_size("band")
    cells = local_cells * devices
    plane = GY * GZ
    depth = local_cells // plane
    ace_scale = 1.0 / math.sqrt(cells * projectors.shape[0])
    window_scale = 1.0 / math.sqrt(cells * band_rows)
    padded = padded_2(response.reshape(band_rows, depth, plane), (("band", 1),), 6)
    padded_wide = padded.astype(jnp.float32).reshape(band_rows, depth + 12, GY, GZ)
    kinetic = -KINETIC * slab_laplacian(padded_wide, depth).reshape(band_rows, local_cells)
    response_wide = response.astype(jnp.float32)
    picked = response
    share = lax.psum_scatter(
        lax.dot_general(picked, projectors, CONTRACT_CELLS, preferred_element_type=jnp.float32),
        "band",
        scatter_dimension=0,
        tiled=True,
    )
    ace_intersection = lax.all_gather(
        (share * ace_scale).astype(jnp.bfloat16), "band", axis=0, tiled=True
    )
    ace_term = -jnp.dot(ace_intersection, projectors, preferred_element_type=jnp.float32)
    applied = (
        kinetic + potential[None, :] * response_wide + ace_term - energies[:, None] * response_wide
    )
    orbitals_wide = orbitals.astype(jnp.float32)
    unprojected = -(perturbing[None, :] * orbitals_wide) - applied
    unprojected_low = unprojected.astype(jnp.bfloat16)
    picked = unprojected_low
    window_share = lax.psum_scatter(
        lax.dot_general(picked, orbitals, CONTRACT_CELLS, preferred_element_type=jnp.float32),
        "band",
        scatter_dimension=0,
        tiled=True,
    )
    window_intersection = lax.all_gather(
        (window_share * window_scale).astype(jnp.bfloat16), "band", axis=0, tiled=True
    )
    block_ids = jnp.arange(band_rows, dtype=jnp.int32) // (band_rows // NBLK)
    lowest = window_start[:, None]
    highest = window_start[:, None] + block_count[:, None] - 1
    inside = (block_ids[None, :] >= lowest) & (block_ids[None, :] <= highest)
    window_intersection = jnp.where(
        inside, window_intersection, jnp.zeros_like(window_intersection)
    )
    residual_wide = unprojected - jnp.dot(
        window_intersection, orbitals, preferred_element_type=jnp.float32
    )
    updated_response = (response_wide + STEP_SIZE * residual_wide).astype(jnp.bfloat16)
    return (updated_response, residual_wide.astype(jnp.bfloat16))


def plane_operator():
    plane = GY * GZ
    op = np.zeros((plane, plane), np.float64)
    for y in range(GY):
        for z in range(GZ):
            out = y * GZ + z
            op[out, out] += 3.0 * COEFFS[0]
            for k in range(1, HALO + 1):
                for sign in (-k, k):
                    op[((y + sign) % GY) * GZ + z, out] += COEFFS[k]
                    op[y * GZ + (z + sign) % GZ, out] += COEFFS[k]
    return (KINETIC * op).astype(np.float32)


def kernel(
    count, groups, ace_scale, window_scale,
    resp_hbm, orb_hbm, proj_hbm, pot, pert, energies, first, blocks, op_hi, op_lo,
    unp_hbm, weights,
    resp, orb, proj, halo_l, halo_r, unp, low, acc, c_send, c_recv, x_send, x_recv, z_send, z_recv, full,
    send_sem, recv_sem, halo_send, halo_recv, load_sem, unp_sem,
):
    rows, cells = resp.shape
    plane = GY * GZ
    depth = cells // plane
    half, quarter = rows // 2, rows // 4
    share = quarter // groups
    chunks = proj.shape[0] // WIDTH

    me = lax.axis_index("band")
    core = me % 2
    across = (me // 2) % 2
    level = me // 4
    left, right = (me + count - 1) % count, (me + 1) % count
    core_peer = me + 1 - 2 * core
    x_peer = me + 2 - 4 * across
    z_levels = [(level + k) % groups for k in range(1, groups)]
    z_peers = [v * 4 + me % 4 for v in z_levels]

    def remote(src, dst, send, recv, device):
        return pltpu.make_async_remote_copy(
            src_ref=src, dst_ref=dst, send_sem=send, recv_sem=recv,
            device_id={"band": device}, device_id_type=pl.DeviceIdType.MESH,
        )

    loads = [pltpu.make_async_copy(resp_hbm, resp, load_sem.at[0])]
    for j in range(chunks):
        at = pl.ds(j * WIDTH, WIDTH)
        loads.append(
            pltpu.make_async_copy(proj_hbm.at[at, :], proj.at[at, :], load_sem.at[1 + j])
        )
    loads.append(pltpu.make_async_copy(orb_hbm, orb, load_sem.at[1 + chunks]))
    for load in loads:
        load.start()

    partners = [left, right, core_peer, x_peer] + z_peers
    barrier = pltpu.get_barrier_semaphore()
    for device in partners:
        pl.semaphore_signal(
            barrier, inc=1, device_id={"band": device}, device_id_type=pl.DeviceIdType.MESH
        )
    loads[0].wait()

    width = HALO * plane
    halos = [
        remote(resp.at[:, cells - width :], halo_l, halo_send.at[0], halo_recv.at[0], right),
        remote(resp.at[:, :width], halo_r, halo_send.at[1], halo_recv.at[1], left),
    ]

    core_row = pl.multiple_of(core * half, half)
    other_row = pl.multiple_of((1 - core) * half, half)
    x_row = pl.multiple_of(core * half + across * quarter, quarter)
    own_row = pl.multiple_of(core * half + across * quarter + level * share, share)
    x_mine = pl.multiple_of(across * quarter, quarter)
    x_other = pl.multiple_of((1 - across) * quarter, quarter)

    nz = groups - 1
    copies = {}

    def begin(j, kind, src, dst, device):
        copy = remote(src, dst, send_sem.at[j, kind], recv_sem.at[j, kind], device)
        copy.start()
        copies[j, kind] = copy

    def partial(j, h, row):
        if j < chunks:
            return lax.dot_general(
                resp[pl.ds(row, half), :], proj[j * WIDTH : (j + 1) * WIDTH, :], NT,
                preferred_element_type=jnp.float32,
            )
        return jnp.concatenate(
            [
                lax.dot_general(
                    low[pl.ds(pl.multiple_of(row + g * quarter, quarter), quarter), :],
                    orb[pl.ds(window(h, g), WIDTH), :], NT,
                    preferred_element_type=jnp.float32,
                )
                for g in range(2)
            ],
            axis=0,
        )

    reach = REACH * (rows // NBLK)

    def window(h, g):
        start = h * (2 * quarter - reach) if g == 0 else quarter - reach + h * (quarter + reach)
        return pl.multiple_of(start, reach)

    def stage_0(j):
        if j < chunks:
            loads[1 + j].wait()
        c_send[j] = partial(j, 1 - core, other_row).astype(jnp.bfloat16)
        if j == 0:
            pl.semaphore_wait(barrier, len(partners))
        begin(j, 0, c_send.at[j], c_recv.at[j], core_peer)
        acc[j] = partial(j, core, core_row)

    def stage_1(j):
        copies[j, 0].wait_recv()
        x_send[j] = (
            acc[j, pl.ds(x_other, quarter), :]
            + c_recv[j, pl.ds(x_other, quarter), :].astype(jnp.float32)
        ).astype(jnp.bfloat16)
        begin(j, 1, x_send.at[j], x_recv.at[j], x_peer)

    def stage_2(j):
        copies[j, 1].wait_recv()
        total = (
            acc[j, pl.ds(x_mine, quarter), :]
            + c_recv[j, pl.ds(x_mine, quarter), :].astype(jnp.float32)
            + x_recv[j].astype(jnp.float32)
        )
        acc[j, :quarter, :] = total
        z_send[j] = total.astype(jnp.bfloat16)
        for k in range(nz):
            begin(
                j, 2 + k,
                z_send.at[j, pl.ds(pl.multiple_of(z_levels[k] * share, share), share), :],
                z_recv.at[j, k], z_peers[k],
            )

    def stage_3(j):
        total = acc[j, pl.ds(pl.multiple_of(level * share, share), share), :]
        for k in range(nz):
            copies[j, 2 + k].wait_recv()
            total = total + z_recv[j, k].astype(jnp.float32)
        scale = ace_scale if j < chunks else window_scale
        full[j, pl.ds(own_row, share), :] = (total * scale).astype(jnp.bfloat16)
        piece = full.at[j, pl.ds(own_row, share), :]
        for k in range(nz):
            begin(j, 2 + nz + k, piece, piece, z_peers[k])

    def stage_4(j):
        for k in range(nz):
            copies[j, 2 + nz + k].wait_recv()
        piece = full.at[j, pl.ds(x_row, quarter), :]
        begin(j, 2 + 2 * nz, piece, piece, x_peer)

    def stage_5(j):
        copies[j, 2 + 2 * nz].wait_recv()
        piece = full.at[j, pl.ds(core_row, half), :]
        begin(j, 3 + 2 * nz, piece, piece, core_peer)

    def stage_6(j):
        copies[j, 3 + 2 * nz].wait_recv()
        if j < chunks:
            for lo in range(0, cells, WIDTH):
                unp[:, lo : lo + WIDTH] += jnp.dot(
                    full[j], proj[j * WIDTH : (j + 1) * WIDTH, lo : lo + WIDTH],
                    preferred_element_type=jnp.float32,
                )

    stages = [stage_0, stage_1, stage_2, stage_3, stage_4, stage_5, stage_6]

    def in_plane():
        for p in range(depth):
            cut = resp[:, p * plane : (p + 1) * plane]
            unp[:, p * plane : (p + 1) * plane] = jnp.dot(
                cut, op_hi[...], preferred_element_type=jnp.float32
            ) + jnp.dot(cut, op_lo[...], preferred_element_type=jnp.float32)

    columns = {}

    def column(ref):
        return jnp.broadcast_to(ref[...].astype(jnp.float32), (plane, rows)).T

    def local_terms(begin_row, end_row):
        @pl.loop(begin_row // ROWS, end_row // ROWS)
        def _(i):
            at = pl.ds(pl.multiple_of(i * ROWS, ROWS), ROWS)
            planes = [
                resp[at, p * plane : (p + 1) * plane].astype(jnp.float32) for p in range(depth)
            ]
            energy = columns["energies"][at, :]
            for p in range(depth):
                cut = slice(p * plane, (p + 1) * plane)
                value = unp[at, cut] + (energy - pot[cut]) * planes[p]
                value = value - pert[cut] * orb[at, cut].astype(jnp.float32)
                for k in range(1, HALO + 1):
                    for q in (p - k, p + k):
                        if 0 <= q < depth:
                            value = value + (KINETIC * COEFFS[k]) * planes[q]
                unp[at, cut] = value

    def halo_terms():
        for copy in halos:
            copy.wait_recv()

        @pl.loop(0, rows // ROWS)
        def _(i):
            at = pl.ds(pl.multiple_of(i * ROWS, ROWS), ROWS)
            before = [
                halo_l[at, p * plane : (p + 1) * plane].astype(jnp.float32) for p in range(HALO)
            ]
            after = [
                halo_r[at, p * plane : (p + 1) * plane].astype(jnp.float32) for p in range(HALO)
            ]
            for p in range(depth):
                value = None
                for k in range(1, HALO + 1):
                    if p - k < 0:
                        term = (KINETIC * COEFFS[k]) * before[HALO + p - k]
                        value = term if value is None else value + term
                    if p + k >= depth:
                        term = (KINETIC * COEFFS[k]) * after[p + k - depth]
                        value = term if value is None else value + term
                if value is not None:
                    unp[at, p * plane : (p + 1) * plane] += value

    slots = chunks + DELAYS[-1]
    halo_slot = chunks + DELAYS[3]
    for t in range(slots):
        if t == 0:
            stage_0(0)
            in_plane()
            acc[chunks, :, :plane] = column(energies)[:half]
            acc[chunks, :, plane : 2 * plane] = column(energies)[half:]
            continue
        for s in range(len(stages) - 1, -1, -1):
            j = t - DELAYS[s]
            if 0 <= j < chunks:
                stages[s](j)
        if t == 1:
            loads[1 + chunks].wait()
        if 1 <= t <= 2:
            columns["energies"] = _HalfView(acc, chunks, (t - 1) * half, plane, t - 1)
            local_terms((t - 1) * half, t * half)
        if t == 3:
            for copy in halos:
                copy.start()
        if t == halo_slot:
            halo_terms()

    unp_copy = pltpu.make_async_copy(unp, unp_hbm, unp_sem)
    unp_copy.start()
    for lo in range(0, rows, quarter):
        low[lo : lo + quarter, :] = unp[lo : lo + quarter, :].astype(jnp.bfloat16)
    for stage in stages[:-1]:
        stage(chunks)

    block = rows // NBLK
    start_col = column(first)
    end_col = start_col + column(blocks)
    insides = []
    for g in range(4):
        at = slice(g * quarter, (g + 1) * quarter)
        start = (0, quarter - reach, 2 * quarter - reach, rows - WIDTH)[g]
        lanes = (lax.broadcasted_iota(jnp.int32, (quarter, plane), 1)).astype(jnp.float32)
        for lo in range(0, WIDTH, plane):
            ids = jnp.floor((lanes + float(start + lo)) * (1.0 / block))
            inside = (ids >= start_col[at]) & (ids < end_col[at])
            insides.append((at, lo, jnp.where(inside, 1.0, 0.0)))
    stages[-1](chunks)
    for at, lo, inside in insides:
        weights[at, lo : lo + plane] = (
            full[chunks, at, lo : lo + plane].astype(jnp.float32) * inside
        ).astype(jnp.bfloat16)
    unp_copy.wait()

    for copy in copies.values():
        copy.wait_send()
    for copy in halos:
        copy.wait_send()


def finish(unp, weights, resp, orb, updated, residual):
    quarter = unp.shape[0]
    rows, cells = orb.shape
    reach = REACH * (rows // NBLK)
    g = pl.program_id(0)
    start = pl.multiple_of(jnp.clip(g * quarter - reach, 0, rows - WIDTH), reach)
    for lo in range(0, cells, WIDTH):
        cut = slice(lo, lo + WIDTH)
        wide = unp[:, cut] - jnp.dot(
            weights[...], orb[pl.ds(start, WIDTH), cut], preferred_element_type=jnp.float32
        )
        residual[:, cut] = wide.astype(jnp.bfloat16)
        updated[:, cut] = (
            resp[:, cut].astype(jnp.float32) + STEP_SIZE * wide
        ).astype(jnp.bfloat16)


class _HalfView:
    def __init__(self, ref, index, offset, plane, part):
        self.ref, self.index, self.offset, self.plane, self.part = ref, index, offset, plane, part

    def __getitem__(self, key):
        at = key[0]
        lo = self.part * self.plane
        return self.ref[
            self.index,
            pl.ds(pl.multiple_of(at.start - self.offset, ROWS), at.size),
            lo : lo + self.plane,
        ]


def shards(
    response, orbitals, projectors, potential, perturbing, energies, window_start, block_count
):
    rows, local = response.shape
    count = lax.axis_size("band")
    cells = local * count
    groups = count // 4
    chunks = projectors.shape[0] // WIDTH
    half, quarter = rows // 2, rows // 4
    share = quarter // groups
    kinds = 4 + 2 * (groups - 1)
    op = plane_operator()
    op_hi = jnp.asarray(op).astype(jnp.bfloat16)
    op_lo = (jnp.asarray(op) - op_hi.astype(jnp.float32)).astype(jnp.bfloat16)
    halo = (rows, HALO * GY * GZ)
    low = jnp.bfloat16
    total = chunks + 1
    vmem = pl.BlockSpec(memory_space=pltpu.VMEM)
    hbm = pl.BlockSpec(memory_space=pl.ANY)
    unprojected, weights = pl.pallas_call(
        functools.partial(
            kernel, count, groups,
            1.0 / math.sqrt(cells * projectors.shape[0]), 1.0 / math.sqrt(cells * rows),
        ),
        out_shape=(
            jax.ShapeDtypeStruct(response.shape, jnp.float32),
            jax.ShapeDtypeStruct((rows, WIDTH), low),
        ),
        in_specs=[hbm] * 3 + [vmem] * 7,
        out_specs=(hbm, vmem),
        scratch_shapes=[
            pltpu.VMEM(response.shape, low),
            pltpu.VMEM(orbitals.shape, low),
            pltpu.VMEM(projectors.shape, low),
            pltpu.VMEM(halo, low),
            pltpu.VMEM(halo, low),
            pltpu.VMEM((rows, local), jnp.float32),
            pltpu.VMEM((rows, local), low),
            pltpu.VMEM((total, half, WIDTH), jnp.float32),
            pltpu.VMEM((total, half, WIDTH), low),
            pltpu.VMEM((total, half, WIDTH), low),
            pltpu.VMEM((total, quarter, WIDTH), low),
            pltpu.VMEM((total, quarter, WIDTH), low),
            pltpu.VMEM((total, quarter, WIDTH), low),
            pltpu.VMEM((total, groups - 1, share, WIDTH), low),
            pltpu.VMEM((total, rows, WIDTH), low),
            pltpu.SemaphoreType.DMA((total, kinds)),
            pltpu.SemaphoreType.DMA((total, kinds)),
            pltpu.SemaphoreType.DMA((2,)),
            pltpu.SemaphoreType.DMA((2,)),
            pltpu.SemaphoreType.DMA((chunks + 2,)),
            pltpu.SemaphoreType.DMA(()),
        ],
        compiler_params=pltpu.CompilerParams(
            collective_id=0, has_side_effects=True, vmem_limit_bytes=56 * 1024 * 1024
        ),
    )(
        response, orbitals, projectors,
        potential, perturbing,
        energies[None, :], window_start[None, :], block_count[None, :],
        op_hi, op_lo,
    )
    band = pl.BlockSpec((quarter, local), lambda g: (g, 0))
    return pl.pallas_call(
        finish,
        out_shape=(jax.ShapeDtypeStruct(response.shape, low),) * 2,
        grid=(4,),
        in_specs=[
            band,
            pl.BlockSpec((quarter, WIDTH), lambda g: (g, 0)),
            band,
            pl.BlockSpec(orbitals.shape, lambda g: (0, 0)),
        ],
        out_specs=(band, band),
        cost_estimate=pl.CostEstimate(
            flops=2 * rows * WIDTH * local, bytes_accessed=12 * rows * local, transcendentals=0
        ),
    )(unprojected, weights, response, orbitals)


def solution(mesh):
    groups = mesh.shape["band"] // 4
    fits = groups * 4 == mesh.shape["band"] and ROW_SHARES % groups == 0
    in_specs = (
        P("pert", "band"),
        P(None, "band"),
        P(None, "band"),
        P("band"),
        P(("pert", "band")),
        P(),
        P(),
        P(),
    )
    out_specs = (P("pert", "band"), P("pert", "band"))
    return jax.shard_map(shards if fits else plain_shards, mesh=mesh, in_specs=in_specs, out_specs=out_specs, check_vma=False)
```

```python
import functools
import math

import jax
import jax.numpy as jnp
import numpy as np
from jax import lax
from jax.experimental import pallas as pl
from jax.experimental.pallas import tpu as pltpu
from jax.sharding import PartitionSpec as P

GY = 8
GZ = 16
NBLK = 32
REACH = 4


COEFFS = (
    -5369.0 / 1800.0,
    12.0 / 7.0,
    -15.0 / 56.0,
    10.0 / 189.0,
    -1.0 / 112.0,
    2.0 / 1925.0,
    -1.0 / 16632.0,
)
KINETIC = 0.125
STEP_SIZE = 0.3
HALO = 6
NT = (((1,), (1,)), ((), ()))
WIDTH = 256
ROWS = 32
ROW_SHARES = 8
PIECE = 128
ORDER = (0, 1, 2, 3, 4, 5, 6)
DELAYS = (0, 1, 3, 5, 7, 9, 10)
HALO_SLOTS = (4, 6)
FINISH = 768


CONTRACT_CELLS = (((1,), (1,)), ((), ()))


def padded_2(cells, sides, width):
    for axis, dim in sides:
        count = lax.axis_size(axis)
        head = lax.slice_in_dim(cells, 0, width, axis=dim)
        tail = lax.slice_in_dim(cells, cells.shape[dim] - width, cells.shape[dim], axis=dim)
        cells = jnp.concatenate(
            [
                lax.ppermute(tail, axis, [(i, (i + 1) % count) for i in range(count)]),
                cells,
                lax.ppermute(head, axis, [((i + 1) % count, i) for i in range(count)]),
            ],
            axis=dim,
        )
    return cells


def slab_laplacian(padded, depth):
    centre = padded[:, 6 : 6 + depth]
    result = 3.0 * COEFFS[0] * centre
    for offset in range(1, 7):
        result = result + COEFFS[offset] * (
            padded[:, 6 + offset : 6 + offset + depth] + padded[:, 6 - offset : 6 - offset + depth]
        )
    for axis_number in (2, 3):
        for offset in range(1, 7):
            result = result + COEFFS[offset] * (
                jnp.roll(centre, offset, axis_number) + jnp.roll(centre, -offset, axis_number)
            )
    return result


def plain_shards(
    response, orbitals, projectors, potential, perturbing, energies, window_start, block_count
):
    band_rows = response.shape[0]
    local_cells = response.shape[1]
    devices = lax.axis_size("band")
    cells = local_cells * devices
    plane = GY * GZ
    depth = local_cells // plane
    ace_scale = 1.0 / math.sqrt(cells * projectors.shape[0])
    window_scale = 1.0 / math.sqrt(cells * band_rows)
    padded = padded_2(response.reshape(band_rows, depth, plane), (("band", 1),), 6)
    padded_wide = padded.astype(jnp.float32).reshape(band_rows, depth + 12, GY, GZ)
    kinetic = -KINETIC * slab_laplacian(padded_wide, depth).reshape(band_rows, local_cells)
    response_wide = response.astype(jnp.float32)
    picked = response
    share = lax.psum_scatter(
        lax.dot_general(picked, projectors, CONTRACT_CELLS, preferred_element_type=jnp.float32),
        "band",
        scatter_dimension=0,
        tiled=True,
    )
    ace_intersection = lax.all_gather(
        (share * ace_scale).astype(jnp.bfloat16), "band", axis=0, tiled=True
    )
    ace_term = -jnp.dot(ace_intersection, projectors, preferred_element_type=jnp.float32)
    applied = (
        kinetic + potential[None, :] * response_wide + ace_term - energies[:, None] * response_wide
    )
    orbitals_wide = orbitals.astype(jnp.float32)
    unprojected = -(perturbing[None, :] * orbitals_wide) - applied
    unprojected_low = unprojected.astype(jnp.bfloat16)
    picked = unprojected_low
    window_share = lax.psum_scatter(
        lax.dot_general(picked, orbitals, CONTRACT_CELLS, preferred_element_type=jnp.float32),
        "band",
        scatter_dimension=0,
        tiled=True,
    )
    window_intersection = lax.all_gather(
        (window_share * window_scale).astype(jnp.bfloat16), "band", axis=0, tiled=True
    )
    block_ids = jnp.arange(band_rows, dtype=jnp.int32) // (band_rows // NBLK)
    lowest = window_start[:, None]
    highest = window_start[:, None] + block_count[:, None] - 1
    inside = (block_ids[None, :] >= lowest) & (block_ids[None, :] <= highest)
    window_intersection = jnp.where(
        inside, window_intersection, jnp.zeros_like(window_intersection)
    )
    residual_wide = unprojected - jnp.dot(
        window_intersection, orbitals, preferred_element_type=jnp.float32
    )
    updated_response = (response_wide + STEP_SIZE * residual_wide).astype(jnp.bfloat16)
    return (updated_response, residual_wide.astype(jnp.bfloat16))


def plane_operator():
    plane = GY * GZ
    op = np.zeros((plane, plane), np.float64)
    for y in range(GY):
        for z in range(GZ):
            out = y * GZ + z
            op[out, out] += 3.0 * COEFFS[0]
            for k in range(1, HALO + 1):
                for sign in (-k, k):
                    op[((y + sign) % GY) * GZ + z, out] += COEFFS[k]
                    op[y * GZ + (z + sign) % GZ, out] += COEFFS[k]
    return (KINETIC * op).astype(np.float32)


def kernel(
    count, groups, ace_scale, window_scale,
    resp_hbm, orb_hbm, proj_hbm, pot, pert, energies, first, blocks, op_hi, op_lo,
    unp_hbm, weights,
    resp, orb, proj, halo_l, halo_r, unp, low, acc, c_send, c_recv, x_send, x_recv, z_send, z_recv, full,
    send_sem, recv_sem, halo_send, halo_recv, load_sem, unp_sem,
):
    rows, cells = resp.shape
    plane = GY * GZ
    depth = cells // plane
    half, quarter = rows // 2, rows // 4
    share = quarter // groups
    chunks = proj.shape[0] // WIDTH

    me = lax.axis_index("band")
    core = me % 2
    across = (me // 2) % 2
    level = me // 4
    left, right = (me + count - 1) % count, (me + 1) % count
    core_peer = me + 1 - 2 * core
    x_peer = me + 2 - 4 * across
    z_levels = [(level + k) % groups for k in range(1, groups)]
    z_peers = [v * 4 + me % 4 for v in z_levels]

    def remote(src, dst, send, recv, device):
        return pltpu.make_async_remote_copy(
            src_ref=src, dst_ref=dst, send_sem=send, recv_sem=recv,
            device_id={"band": device}, device_id_type=pl.DeviceIdType.MESH,
        )

    loads = [pltpu.make_async_copy(resp_hbm, resp, load_sem.at[0])]
    for j in range(chunks):
        at = pl.ds(j * WIDTH, WIDTH)
        loads.append(
            pltpu.make_async_copy(proj_hbm.at[at, :], proj.at[at, :], load_sem.at[1 + j])
        )
    loads.append(pltpu.make_async_copy(orb_hbm, orb, load_sem.at[1 + chunks]))
    for load in loads:
        load.start()

    partners = [left, right, core_peer, x_peer] + z_peers
    barrier = pltpu.get_barrier_semaphore()
    for device in partners:
        pl.semaphore_signal(
            barrier, inc=1, device_id={"band": device}, device_id_type=pl.DeviceIdType.MESH
        )
    loads[0].wait()

    width = HALO * plane
    halos = [
        remote(resp.at[:, cells - width :], halo_l, halo_send.at[0], halo_recv.at[0], right),
        remote(resp.at[:, :width], halo_r, halo_send.at[1], halo_recv.at[1], left),
    ]

    core_row = pl.multiple_of(core * half, half)
    other_row = pl.multiple_of((1 - core) * half, half)
    x_row = pl.multiple_of(core * half + across * quarter, quarter)
    own_row = pl.multiple_of(core * half + across * quarter + level * share, share)
    x_mine = pl.multiple_of(across * quarter, quarter)
    x_other = pl.multiple_of((1 - across) * quarter, quarter)

    nz = groups - 1
    copies = {}

    def begin(j, kind, src, dst, device):
        copy = remote(src, dst, send_sem.at[j, kind], recv_sem.at[j, kind], device)
        copy.start()
        copies[j, kind] = copy

    def cols(j):
        return slice(0, WIDTH if j < chunks else PIECE)

    def partial(j, h, row):
        if j < chunks:
            return lax.dot_general(
                resp[pl.ds(row, half), :], proj[j * WIDTH : (j + 1) * WIDTH, :], NT,
                preferred_element_type=jnp.float32,
            )
        return jnp.concatenate(
            [
                lax.dot_general(
                    low[pl.ds(pl.multiple_of(row + g * quarter, quarter), quarter), :],
                    orb[pl.ds(window(h, g) + (j - chunks) * PIECE, PIECE), :], NT,
                    preferred_element_type=jnp.float32,
                )
                for g in range(2)
            ],
            axis=0,
        )

    reach = REACH * (rows // NBLK)

    def window(h, g):
        start = h * (2 * quarter - reach) if g == 0 else quarter - reach + h * (quarter + reach)
        return pl.multiple_of(start, reach)

    def stage_0(j):
        if j < chunks:
            loads[1 + j].wait()
        w = cols(j)
        c_send[j, :, w] = partial(j, 1 - core, other_row).astype(jnp.bfloat16)
        if j == 0:
            pl.semaphore_wait(barrier, len(partners))
        begin(j, 0, c_send.at[j, :, w], c_recv.at[j, :, w], core_peer)
        acc[j, :, w] = partial(j, core, core_row)

    def stage_1(j):
        w = cols(j)
        copies[j, 0].wait_recv()
        x_send[j, :, w] = (
            acc[j, pl.ds(x_other, quarter), w]
            + c_recv[j, pl.ds(x_other, quarter), w].astype(jnp.float32)
        ).astype(jnp.bfloat16)
        begin(j, 1, x_send.at[j, :, w], x_recv.at[j, :, w], x_peer)

    def stage_2(j):
        w = cols(j)
        copies[j, 1].wait_recv()
        total = (
            acc[j, pl.ds(x_mine, quarter), w]
            + c_recv[j, pl.ds(x_mine, quarter), w].astype(jnp.float32)
            + x_recv[j, :, w].astype(jnp.float32)
        )
        acc[j, :quarter, w] = total
        z_send[j, :, w] = total.astype(jnp.bfloat16)
        for k in range(nz):
            begin(
                j, 2 + k,
                z_send.at[j, pl.ds(pl.multiple_of(z_levels[k] * share, share), share), w],
                z_recv.at[j, k, :, w], z_peers[k],
            )

    def stage_3(j):
        w = cols(j)
        total = acc[j, pl.ds(pl.multiple_of(level * share, share), share), w]
        for k in range(nz):
            copies[j, 2 + k].wait_recv()
            total = total + z_recv[j, k, :, w].astype(jnp.float32)
        scale = ace_scale if j < chunks else window_scale
        full[j, pl.ds(own_row, share), w] = (total * scale).astype(jnp.bfloat16)
        piece = full.at[j, pl.ds(own_row, share), w]
        for k in range(nz):
            begin(j, 2 + nz + k, piece, piece, z_peers[k])

    def stage_4(j):
        for k in range(nz):
            copies[j, 2 + nz + k].wait_recv()
        piece = full.at[j, pl.ds(x_row, quarter), cols(j)]
        begin(j, 2 + 2 * nz, piece, piece, x_peer)

    def stage_5(j):
        copies[j, 2 + 2 * nz].wait_recv()
        piece = full.at[j, pl.ds(core_row, half), cols(j)]
        begin(j, 3 + 2 * nz, piece, piece, core_peer)

    def stage_6(j):
        copies[j, 3 + 2 * nz].wait_recv()
        if j < chunks:
            for lo in range(0, cells, WIDTH):
                unp[:, lo : lo + WIDTH] += jnp.dot(
                    full[j], proj[j * WIDTH : (j + 1) * WIDTH, lo : lo + WIDTH],
                    preferred_element_type=jnp.float32,
                )

    stages = [stage_0, stage_1, stage_2, stage_3, stage_4, stage_5, stage_6]

    def in_plane():
        for p in range(depth):
            cut = resp[:, p * plane : (p + 1) * plane]
            unp[:, p * plane : (p + 1) * plane] = jnp.dot(
                cut, op_hi[...], preferred_element_type=jnp.float32
            ) + jnp.dot(cut, op_lo[...], preferred_element_type=jnp.float32)

    columns = {}

    def column(ref):
        return jnp.broadcast_to(ref[...].astype(jnp.float32), (plane, rows)).T

    def local_terms(begin_row, end_row):
        @pl.loop(begin_row // ROWS, end_row // ROWS)
        def _(i):
            at = pl.ds(pl.multiple_of(i * ROWS, ROWS), ROWS)
            planes = [
                resp[at, p * plane : (p + 1) * plane].astype(jnp.float32) for p in range(depth)
            ]
            energy = columns["energies"][at, :]
            for p in range(depth):
                cut = slice(p * plane, (p + 1) * plane)
                value = unp[at, cut] + (energy - pot[cut]) * planes[p]
                value = value - pert[cut] * orb[at, cut].astype(jnp.float32)
                for k in range(1, HALO + 1):
                    for q in (p - k, p + k):
                        if 0 <= q < depth:
                            value = value + (KINETIC * COEFFS[k]) * planes[q]
                unp[at, cut] = value

    def halo_terms():
        for copy in halos:
            copy.wait_recv()

        @pl.loop(0, rows // ROWS)
        def _(i):
            at = pl.ds(pl.multiple_of(i * ROWS, ROWS), ROWS)
            before = [
                halo_l[at, p * plane : (p + 1) * plane].astype(jnp.float32) for p in range(HALO)
            ]
            after = [
                halo_r[at, p * plane : (p + 1) * plane].astype(jnp.float32) for p in range(HALO)
            ]
            for p in range(depth):
                value = None
                for k in range(1, HALO + 1):
                    if p - k < 0:
                        term = (KINETIC * COEFFS[k]) * before[HALO + p - k]
                        value = term if value is None else value + term
                    if p + k >= depth:
                        term = (KINETIC * COEFFS[k]) * after[p + k - depth]
                        value = term if value is None else value + term
                if value is not None:
                    unp[at, p * plane : (p + 1) * plane] += value

    slots = chunks + DELAYS[-1]
    halo_slot = chunks + DELAYS[3]
    for t in range(slots):
        if t == 0:
            stage_0(0)
            in_plane()
            acc[chunks, :, :plane] = column(energies)[:half]
            acc[chunks, :, plane : 2 * plane] = column(energies)[half:]
            continue
        for s in ORDER:
            j = t - DELAYS[s]
            if 0 <= j < chunks:
                stages[s](j)
        if t == 1:
            loads[1 + chunks].wait()
        if 1 <= t <= 2:
            columns["energies"] = _HalfView(acc, chunks, (t - 1) * half, plane, t - 1)
            local_terms((t - 1) * half, t * half)
        for slot, copy in zip(HALO_SLOTS, halos):
            if t == slot:
                copy.start()
        if t == halo_slot:
            halo_terms()

    unp_copy = pltpu.make_async_copy(unp, unp_hbm, unp_sem)
    unp_copy.start()
    for lo in range(0, rows, quarter):
        low[lo : lo + quarter, :] = unp[lo : lo + quarter, :].astype(jnp.bfloat16)
    for stage in stages[:-1]:
        for j in range(chunks, chunks + WIDTH // PIECE):
            stage(j)

    block = rows // NBLK
    start_col = column(first)
    end_col = start_col + column(blocks)
    insides = []
    for g in range(4):
        at = slice(g * quarter, (g + 1) * quarter)
        start = (0, quarter - reach, 2 * quarter - reach, rows - WIDTH)[g]
        lanes = (lax.broadcasted_iota(jnp.int32, (quarter, plane), 1)).astype(jnp.float32)
        for lo in range(0, WIDTH, plane):
            ids = jnp.floor((lanes + float(start + lo)) * (1.0 / block))
            inside = (ids >= start_col[at]) & (ids < end_col[at])
            insides.append((at, lo, jnp.where(inside, 1.0, 0.0)))
    for j in range(chunks, chunks + WIDTH // PIECE):
        stages[-1](j)
    for at, lo, inside in insides:
        weights[at, lo : lo + plane] = (
            full[chunks + lo // PIECE, at, :PIECE].astype(jnp.float32) * inside
        ).astype(jnp.bfloat16)
    unp_copy.wait()

    for copy in copies.values():
        copy.wait_send()
    for copy in halos:
        copy.wait_send()


def finish(unp, weights, resp, orb, updated, residual):
    rows = orb.shape[0]
    quarter = rows // 4
    reach = REACH * (rows // NBLK)
    for g in range(4):
        at = slice(g * quarter, (g + 1) * quarter)
        start = min(max(g * quarter - reach, 0), rows - WIDTH)
        wide = unp[at, :] - jnp.dot(
            weights[at, :], orb[start : start + WIDTH, :], preferred_element_type=jnp.float32
        )
        residual[at, :] = wide.astype(jnp.bfloat16)
        updated[at, :] = (resp[at, :].astype(jnp.float32) + STEP_SIZE * wide).astype(jnp.bfloat16)


class _HalfView:
    def __init__(self, ref, index, offset, plane, part):
        self.ref, self.index, self.offset, self.plane, self.part = ref, index, offset, plane, part

    def __getitem__(self, key):
        at = key[0]
        lo = self.part * self.plane
        return self.ref[
            self.index,
            pl.ds(pl.multiple_of(at.start - self.offset, ROWS), at.size),
            lo : lo + self.plane,
        ]


def shards(
    response, orbitals, projectors, potential, perturbing, energies, window_start, block_count
):
    rows, local = response.shape
    count = lax.axis_size("band")
    cells = local * count
    groups = count // 4
    chunks = projectors.shape[0] // WIDTH
    half, quarter = rows // 2, rows // 4
    share = quarter // groups
    kinds = 4 + 2 * (groups - 1)
    op = plane_operator()
    op_hi = jnp.asarray(op).astype(jnp.bfloat16)
    op_lo = (jnp.asarray(op) - op_hi.astype(jnp.float32)).astype(jnp.bfloat16)
    halo = (rows, HALO * GY * GZ)
    low = jnp.bfloat16
    total = chunks + WIDTH // PIECE
    vmem = pl.BlockSpec(memory_space=pltpu.VMEM)
    hbm = pl.BlockSpec(memory_space=pl.ANY)
    unprojected, weights = pl.pallas_call(
        functools.partial(
            kernel, count, groups,
            1.0 / math.sqrt(cells * projectors.shape[0]), 1.0 / math.sqrt(cells * rows),
        ),
        out_shape=(
            jax.ShapeDtypeStruct(response.shape, jnp.float32),
            jax.ShapeDtypeStruct((rows, WIDTH), low),
        ),
        in_specs=[hbm] * 3 + [vmem] * 7,
        out_specs=(hbm, vmem),
        scratch_shapes=[
            pltpu.VMEM(response.shape, low),
            pltpu.VMEM(orbitals.shape, low),
            pltpu.VMEM(projectors.shape, low),
            pltpu.VMEM(halo, low),
            pltpu.VMEM(halo, low),
            pltpu.VMEM((rows, local), jnp.float32),
            pltpu.VMEM((rows, local), low),
            pltpu.VMEM((total, half, WIDTH), jnp.float32),
            pltpu.VMEM((total, half, WIDTH), low),
            pltpu.VMEM((total, half, WIDTH), low),
            pltpu.VMEM((total, quarter, WIDTH), low),
            pltpu.VMEM((total, quarter, WIDTH), low),
            pltpu.VMEM((total, quarter, WIDTH), low),
            pltpu.VMEM((total, groups - 1, share, WIDTH), low),
            pltpu.VMEM((total, rows, WIDTH), low),
            pltpu.SemaphoreType.DMA((total, kinds)),
            pltpu.SemaphoreType.DMA((total, kinds)),
            pltpu.SemaphoreType.DMA((2,)),
            pltpu.SemaphoreType.DMA((2,)),
            pltpu.SemaphoreType.DMA((chunks + 2,)),
            pltpu.SemaphoreType.DMA(()),
        ],
        compiler_params=pltpu.CompilerParams(
            collective_id=0, has_side_effects=True, vmem_limit_bytes=56 * 1024 * 1024
        ),
    )(
        response, orbitals, projectors,
        potential, perturbing,
        energies[None, :], window_start[None, :], block_count[None, :],
        op_hi, op_lo,
    )
    band = pl.BlockSpec((rows, FINISH), lambda g: (0, g))
    return pl.pallas_call(
        finish,
        out_shape=(jax.ShapeDtypeStruct(response.shape, low),) * 2,
        grid=(local // FINISH,),
        in_specs=[band, pl.BlockSpec((rows, WIDTH), lambda g: (0, 0)), band, band],
        out_specs=(band, band),
        cost_estimate=pl.CostEstimate(
            flops=2 * rows * WIDTH * local, bytes_accessed=12 * rows * local, transcendentals=0
        ),
    )(unprojected, weights, response, orbitals)


def solution(mesh):
    groups = mesh.shape["band"] // 4
    fits = groups * 4 == mesh.shape["band"] and ROW_SHARES % groups == 0
    in_specs = (
        P("pert", "band"),
        P(None, "band"),
        P(None, "band"),
        P("band"),
        P(("pert", "band")),
        P(),
        P(),
        P(),
    )
    out_specs = (P("pert", "band"), P("pert", "band"))
    return jax.shard_map(shards if fits else plain_shards, mesh=mesh, in_specs=in_specs, out_specs=out_specs, check_vma=False)
```
